32 devices in a mesh: groups: 2 (over y), sec: 2 (over x), row: 4 (over z), col: 2 (over core).
Axes of the slice: x: 2, y: 2, z: 4, core: 2. Of those that a mesh axis runs over, the one named last changes fastest.
Arguments:
- factors: bfloat16 [4, 2048, 2048], P(('groups', 'sec'), 'row', 'col'), parts along dimension 0, may hold values from -0.125 to 0.125
- inverses: bfloat16 [4, 2048, 2048], P(('groups', 'sec'), 'row', 'col'), parts along dimension 0, may hold values from -1.4 to 1.4, as said below
- sigma_end: float32 [4096, 2048], P(('groups', 'row'), 'col'), parts along dimension 0, may hold values from -1 to 6, as said below
Outputs:
- variance: float32 [4, 2048, 2048], P(('groups', 'sec'), 'row', 'col'), parts along dimension 0
The draws below stay inside these ranges and needn't reach their ends.
There are 2 independent parts, one for each index of `groups`. The reference program is written for one: setup_inputs(seed, part) draws one part's arguments, and reference() takes and returns one part's arrays. A program takes and returns all parts, laid end to end along the dimension named above; each array names one. Nothing has to cross between parts.
Inputs may be any that keep to these rules, and one draw needn't show every extreme that they name: inverses[t] is lower triangular; its diagonal entries lie in 0.6 to 1.4. sigma_end is symmetric with diagonal entries in 2.5 to 6.
All inputs are finite; a program needn't handle non-finite values.
Results may differ from the reference program's by a relative error of at most 0.011.
Values may be sent and summed in bfloat16 or wider, within the bound.
A program may use at most 64 MiB of HBM per device.

```python
import math
import jax
import jax.numpy as jnp
from jax import lax

B = 2048
STEPS = 2


def draw_inverses(key, part):
    first_key, second_key = jax.random.split(jax.random.fold_in(key, 7))
    shape = (STEPS, B, B)
    below = jnp.clip(jax.random.normal(first_key, shape, jnp.float32) * 0.7, -2.8, 2.8)
    below = below / math.sqrt(B)
    diag_values = jax.random.uniform(second_key, (STEPS, 1, B), jnp.float32, 0.6, 1.4)
    row_ids = lax.broadcasted_iota(jnp.int32, (1, B, B), 1)
    col_ids = lax.broadcasted_iota(jnp.int32, (1, B, B), 2)
    lower = jnp.where(col_ids < row_ids, below, 0.0) + jnp.where(col_ids == row_ids, diag_values, 0.0)
    return lower.astype(jnp.bfloat16)


def draw_sigma_end(key, part):
    first_key, second_key = jax.random.split(jax.random.fold_in(key, 13))
    raw = jnp.clip(jax.random.normal(first_key, (B, B), jnp.float32), -4.0, 4.0)
    raw = raw / math.sqrt(B)
    symmetric = 0.5 * (raw + raw.T)
    diag_values = jax.random.uniform(second_key, (1, B), jnp.float32, 2.5, 6.0)
    row_ids = lax.broadcasted_iota(jnp.int32, (B, B), 0)
    col_ids = lax.broadcasted_iota(jnp.int32, (B, B), 1)
    return jnp.where(row_ids == col_ids, diag_values, symmetric).astype(jnp.float32)


def block_scale(stream_key, shape, cuts, smallest, largest):
    def one(dim, blocks):
        draws = jax.random.uniform(jax.random.fold_in(jax.random.fold_in(stream_key, 6), dim), (blocks,), jnp.float32, smallest / len(cuts), largest / len(cuts))
        return jnp.repeat(jnp.exp(draws), shape[dim] // blocks).reshape((-1,) + (1,) * (len(shape) - dim - 1))

    level = one(*cuts[0])
    for cut in cuts[1:]:
        level = level * one(*cut)
    return level


def noise(rng, dims, width, bound, shards=(), dtype=jnp.bfloat16):
    array = width * jax.random.normal(rng, dims, jnp.float32)
    if shards:
        array = array * block_scale(rng, dims, shards, -0.22, 0.18)
    return jnp.clip(array, -bound, bound).astype(dtype)


def setup_inputs(seed: int = 0, part: int = 0) -> dict:
    arg_keys = jax.random.split(jax.random.key(seed), 4)
    part_splits = jax.random.split(jax.random.fold_in(arg_keys[3], part), 4)
    factors = noise(part_splits[0], (STEPS, B, B), B ** -0.5, 0.125, ((0, 2), (1, 4), (2, 2)))
    inverses = draw_inverses(jax.random.fold_in(jax.random.fold_in(arg_keys[3], part), 71), part)
    sigma_end = draw_sigma_end(jax.random.fold_in(jax.random.fold_in(arg_keys[3], part), 71), part)
    return dict(factors=factors, inverses=inverses, sigma_end=sigma_end)


def reference(factors, inverses, sigma_end):
    count = factors.shape[0]
    state = sigma_end
    produced = []
    for position in range(count - 1, -1, -1):
        inverse_now = inverses[position]
        diag_term = jnp.dot(inverse_now.T, inverse_now, preferred_element_type=jnp.float32)
        state_low = state.astype(jnp.bfloat16)
        image = jnp.dot(state_low, factors[position], preferred_element_type=jnp.float32).astype(jnp.bfloat16)
        result = diag_term + jnp.dot(factors[position].T, image, preferred_element_type=jnp.float32)
        produced.append(result)
        state = result
    return jnp.stack(produced[::-1])
```

```python
import jax
import jax.numpy as jnp
from jax import lax
from jax.sharding import PartitionSpec as P


def partner(shard, axis, stride):
    return lax.ppermute(shard, axis, [(i, i ^ 1 << stride) for i in range(lax.axis_size(axis))])


def passed_along(value, axis, steps):
    count = lax.axis_size(axis)
    first, last = (max(0, -steps), min(count, count - steps))
    return lax.ppermute(value, axis, [(source, source + steps) for source in range(first, last)])


def local(factors, inverses, sigma_end):
    row_size = lax.axis_size("row")
    col_size = lax.axis_size("col")
    sec_size = lax.axis_size("sec")
    row_index = lax.axis_index("row")
    col_index = lax.axis_index("col")
    sec_index = lax.axis_index("sec")
    _, tile_rows, _ = factors.shape
    per_column = row_size // col_size
    offset = row_index % per_column * tile_rows
    owns_panel = col_index == row_index // per_column

    def gather(tile):
        return lax.all_gather(tile, "row", axis=0, tiled=True)

    def left_of(full):
        mine = lax.dynamic_slice_in_dim(full, offset, tile_rows, 1)
        return jnp.where(owns_panel, mine, partner(mine, "col", 0))

    def cross(left, full):
        return lax.dot_general(
            left, full, (((0,), (0,)), ((), ())), preferred_element_type=jnp.float32
        )

    current = sigma_end.astype(jnp.bfloat16)
    factor = gather(factors[0])
    state = gather(current)
    inverse = gather(inverses[0])
    factor_left = left_of(factor)
    diagonal = cross(left_of(inverse), inverse)
    result = None
    for segment in range(sec_size):
        half = cross(factor_left, state).astype(jnp.bfloat16)
        whole = lax.all_gather(half, "col", axis=1, tiled=True)
        block = diagonal + jnp.dot(whole, factor, preferred_element_type=jnp.float32)
        active = sec_index == sec_size - 1 - segment
        result = block if result is None else jnp.where(active, block, result)
        if segment < sec_size - 1:
            state = gather(passed_along(block.astype(jnp.bfloat16), "sec", -1))
    return result[None]


def solution(mesh):
    in_specs = (
        P(("groups", "sec"), "row", "col"),
        P(("groups", "sec"), "row", "col"),
        P(("groups", "row"), "col"),
    )
    out_specs = P(("groups", "sec"), "row", "col")
    return jax.shard_map(local, mesh=mesh, in_specs=in_specs, out_specs=out_specs, check_vma=False)
```

```python
import jax
import jax.numpy as jnp
from jax import lax
from jax.experimental import pallas as pl
from jax.experimental.pallas import tpu as pltpu
from jax.sharding import PartitionSpec as P


def partner(shard, axis, stride):
    return lax.ppermute(shard, axis, [(i, i ^ 1 << stride) for i in range(lax.axis_size(axis))])


def passed_along(value, axis, steps):
    count = lax.axis_size(axis)
    first, last = (max(0, -steps), min(count, count - steps))
    return lax.ppermute(value, axis, [(source, source + steps) for source in range(first, last)])


def local(factors, inverses, sigma_end):
    row_size = lax.axis_size("row")
    col_size = lax.axis_size("col")
    sec_size = lax.axis_size("sec")
    row_index = lax.axis_index("row")
    col_index = lax.axis_index("col")
    sec_index = lax.axis_index("sec")
    _, tile_rows, _ = factors.shape
    per_column = row_size // col_size
    offset = row_index % per_column * tile_rows
    owns_panel = col_index == row_index // per_column

    def gather(tile):
        return lax.all_gather(tile, "row", axis=0, tiled=True)

    def left_of(full):
        mine = lax.dynamic_slice_in_dim(full, offset, tile_rows, 1)
        return jnp.where(owns_panel, mine, partner(mine, "col", 0))

    def cross(left, full):
        return lax.dot_general(
            left, full, (((0,), (0,)), ((), ())), preferred_element_type=jnp.float32
        )

    current = sigma_end.astype(jnp.bfloat16)
    factor = gather(factors[0])
    state = gather(current)
    inverse = gather(inverses[0])
    factor_left = left_of(factor)
    diagonal = cross(left_of(inverse), inverse)
    result = None
    for segment in range(sec_size):
        half = cross(factor_left, state).astype(jnp.bfloat16)
        whole = lax.all_gather(half, "col", axis=1, tiled=True)
        block = diagonal + jnp.dot(whole, factor, preferred_element_type=jnp.float32)
        active = sec_index == sec_size - 1 - segment
        result = block if result is None else jnp.where(active, block, result)
        if segment < sec_size - 1:
            state = gather(passed_along(block.astype(jnp.bfloat16), "sec", -1))
    return result[None]


FAC, INV, SIG, STA = range(4)
DOWN, UP = range(2)
MESH = pl.DeviceIdType.MESH
TA = (((0,), (0,)), ((), ()))


def kernel(n, f_ref, g_ref, s_ref, out, fb, gb, sb, xb, fl, gl, zb, ssem, rsem, hop_s, hop_x, left_s, left_r, z_s, z_r):
    r = lax.axis_index("row")
    c = lax.axis_index("col")
    sec = lax.axis_index("sec")
    t = f_ref.shape[1]
    lower, upper = r > 0, r < n - 1
    bufs = {FAC: fb, INV: gb, SIG: sb, STA: xb}
    lefts = (fl, gl)
    owner = c == r // 2
    hl = r % 2

    barrier = pltpu.get_barrier_semaphore()
    pl.semaphore_signal(barrier, inc=1, device_id={"col": 1 - c}, device_id_type=MESH)
    pl.semaphore_signal(barrier, inc=1, device_id={"sec": 1 - sec}, device_id_type=MESH)

    @pl.when(lower)
    def _():
        pl.semaphore_signal(barrier, inc=1, device_id={"row": r - 1}, device_id_type=MESH)

    @pl.when(upper)
    def _():
        pl.semaphore_signal(barrier, inc=1, device_id={"row": r + 1}, device_id_type=MESH)

    pl.semaphore_wait(barrier, 2 + lower.astype(jnp.int32) + upper.astype(jnp.int32))

    def rows(k):
        return pl.ds(pl.multiple_of(k * t, t), t)

    def cols(h):
        return pl.ds(h * t, t)

    def along(a, k, h, way):
        piece = bufs[a].at[h, rows(k), :]
        to = r - 1 if way == DOWN else r + 1
        return pltpu.make_async_remote_copy(
            src_ref=piece,
            dst_ref=piece,
            send_sem=ssem.at[a, h, k, way],
            recv_sem=rsem.at[a, h, k],
            device_id={"row": to},
            device_id_type=MESH,
        )

    def hop_sigma(k):
        piece = sb.at[0, rows(k), :]
        return pltpu.make_async_remote_copy(
            src_ref=piece, dst_ref=piece, send_sem=hop_s.at[k], recv_sem=rsem.at[SIG, 0, k],
            device_id={"sec": 1}, device_id_type=MESH,
        )

    def hop_state(h):
        piece = xb.at[h, rows(r), :]
        return pltpu.make_async_remote_copy(
            src_ref=piece, dst_ref=piece, send_sem=hop_x.at[h], recv_sem=rsem.at[STA, h, r],
            device_id={"sec": 0}, device_id_type=MESH,
        )

    def to_left(a, k):
        return pltpu.make_async_remote_copy(
            src_ref=bufs[a].at[hl, rows(k), :], dst_ref=lefts[a].at[rows(k), :],
            send_sem=left_s.at[a, k], recv_sem=left_r.at[a, k],
            device_id={"col": 1 - c}, device_id_type=MESH,
        )

    def flows(a, k, h, way):
        if a != INV:
            return True
        return (2 * c + h <= k) if way == DOWN else False

    def when(*terms):
        total = True
        for term in terms:
            if term is False:
                return lambda f: None
            if term is not True:
                total = term if total is True else jnp.logical_and(total, term)
        return pl.when(total)

    def start_own(a, h):
        @when(lower, flows(a, r, h, DOWN))
        def _():
            along(a, r, h, DOWN).start()

        @when(upper, flows(a, r, h, UP))
        def _():
            along(a, r, h, UP).start()

    def receive(a, h, d, then=None):
        for way, k, edge in ((DOWN, r + d, lower), (UP, r - d, upper)):
            @when(k < n if way == DOWN else k >= 0, flows(a, k, h, way))
            def _():
                along(a, k, h, way).wait_recv()

                @pl.when(edge)
                def _():
                    along(a, k, h, way).start()

                if then is not None:
                    then(k)

    def finish(a, h, ways=(DOWN, UP)):
        for k in range(n):
            for way in ways:
                side = jnp.logical_and(lower, r <= k) if way == DOWN else jnp.logical_and(upper, r >= k)

                @when(side, flows(a, k, h, way))
                def _():
                    along(a, k, h, way).wait_send()

    def share_left(a, k):
        @pl.when(owner)
        def _():
            to_left(a, k).start()
            lefts[a][rows(k), :] = bufs[a][hl, rows(k), :]

    for h in range(2):
        sb[h, rows(r), :] = s_ref[:, cols(h)].astype(jnp.bfloat16)
    start_own(SIG, sec)
    for h in range(2):
        fb[h, rows(r), :] = f_ref[0, :, cols(h)]
        start_own(FAC, h)
    for h in range(2):
        gb[h, rows(r), :] = g_ref[0, :, cols(h)]
        start_own(INV, h)
    share_left(FAC, r)
    share_left(INV, r)

    for k in range(n):
        @pl.when(k < r)
        def _():
            gl[rows(k), :] = jnp.zeros((t, t), jnp.bfloat16)
        for h in range(2):
            @pl.when(jnp.logical_or(k < r, jnp.logical_and(k != r, k < 2 * c + h)))
            def _():
                gb[h, rows(k), :] = jnp.zeros((t, t), jnp.bfloat16)

    def pass_sigma(k):
        @pl.when(sec == 0)
        def _():
            hop_sigma(k).start()

    for d in range(1, n):
        receive(SIG, sec, d, pass_sigma)
        for h in range(2):
            receive(FAC, h, d)
        for k, inside in ((r + d, r + d < n), (r - d, r - d >= 0)):
            @pl.when(inside)
            def _():
                share_left(FAC, k)
        for h in range(2):
            receive(INV, h, d)

        @pl.when(r + d < n)
        def _():
            share_left(INV, r + d)

    @pl.when(jnp.logical_not(owner))
    def _():
        for k in range(n):
            to_left(FAC, k).wait_recv()

            @pl.when(k >= r)
            def _():
                to_left(INV, k).wait_recv()

    for h in range(2):
        out[0, :, cols(h)] = lax.dot_general(gl[...], gb[h], TA, preferred_element_type=jnp.float32)

    def send_z():
        piece = zb.at[c]
        return pltpu.make_async_remote_copy(
            src_ref=piece, dst_ref=piece, send_sem=z_s, recv_sem=z_r,
            device_id={"col": 1 - c}, device_id_type=MESH,
        )

    def products(buf, then):
        for h in range(2):
            zb[c, :, cols(h)] = lax.dot_general(
                fl[...], buf[h], TA, preferred_element_type=jnp.float32
            ).astype(jnp.bfloat16)
        send_z().start()
        send_z().wait_recv()
        for h in range(2):
            total = out[0, :, cols(h)]
            for j in range(2):
                total += jnp.dot(zb[j], fb[h, j * 2 * t:(j + 1) * 2 * t, :], preferred_element_type=jnp.float32)
            out[0, :, cols(h)] = total
            then(h, total)

    @pl.when(sec == 1)
    def _():
        for k in range(n):
            @pl.when(k != r)
            def _():
                hop_sigma(k).wait_recv()

        def onward(h, total):
            xb[h, rows(r), :] = total.astype(jnp.bfloat16)
            hop_state(h).start()

        products(sb, onward)
        for h in range(2):
            hop_state(h).wait_send()

    @pl.when(sec == 0)
    def _():
        for h in range(2):
            hop_state(h).wait_recv()
            start_own(STA, h)
        for d in range(1, n):
            for h in range(2):
                receive(STA, h, d)
        products(xb, lambda h, total: None)
        for h in range(2):
            finish(STA, h)
        for k in range(n):
            @pl.when(k != r)
            def _():
                hop_sigma(k).wait_send()

    send_z().wait_send()
    finish(SIG, sec)
    for h in range(2):
        finish(FAC, h)
        finish(INV, h, (DOWN,))

    @pl.when(owner)
    def _():
        for k in range(n):
            to_left(FAC, k).wait_send()

            @pl.when(k >= r)
            def _():
                to_left(INV, k).wait_send()


def fused(factors, inverses, sigma_end):
    n = lax.axis_size("row")
    _, t, width = factors.shape
    low = jnp.bfloat16
    dma = pltpu.SemaphoreType.DMA
    vmem = pl.BlockSpec(memory_space=pltpu.VMEM)
    wide = pltpu.VMEM((2, n * t, t), low)
    return pl.pallas_call(
        lambda *refs: kernel(n, *refs),
        out_shape=jax.ShapeDtypeStruct((1, t, width), jnp.float32),
        in_specs=[vmem] * 3,
        out_specs=vmem,
        scratch_shapes=[
            wide, wide, wide, wide,
            pltpu.VMEM((n * t, t), low),
            pltpu.VMEM((n * t, t), low),
            pltpu.VMEM((2, t, 2 * t), low),
            dma((4, 2, n, 2)), dma((4, 2, n)), dma((n,)), dma((2,)),
            dma((2, n)), dma((2, n)), dma(()), dma(()),
        ],
        compiler_params=pltpu.CompilerParams(
            collective_id=0, has_side_effects=True, vmem_limit_bytes=56 * 2**20
        ),
    )(factors, inverses, sigma_end)


def solution(mesh):
    in_specs = (
        P(("groups", "sec"), "row", "col"),
        P(("groups", "sec"), "row", "col"),
        P(("groups", "row"), "col"),
    )
    fits = mesh.shape["sec"] == 2 and mesh.shape["row"] == 2 * mesh.shape["col"] == 4
    body = fused if fits else local
    out_specs = P(("groups", "sec"), "row", "col")
    return jax.shard_map(body, mesh=mesh, in_specs=in_specs, out_specs=out_specs, check_vma=False)
```

```python
import jax
import jax.numpy as jnp
from jax import lax
from jax.experimental import pallas as pl
from jax.experimental.pallas import tpu as pltpu
from jax.sharding import PartitionSpec as P


def partner(shard, axis, stride):
    return lax.ppermute(shard, axis, [(i, i ^ 1 << stride) for i in range(lax.axis_size(axis))])


def passed_along(value, axis, steps):
    count = lax.axis_size(axis)
    first, last = (max(0, -steps), min(count, count - steps))
    return lax.ppermute(value, axis, [(source, source + steps) for source in range(first, last)])


def local(factors, inverses, sigma_end):
    row_size = lax.axis_size("row")
    col_size = lax.axis_size("col")
    sec_size = lax.axis_size("sec")
    row_index = lax.axis_index("row")
    col_index = lax.axis_index("col")
    sec_index = lax.axis_index("sec")
    _, tile_rows, _ = factors.shape
    per_column = row_size // col_size
    offset = row_index % per_column * tile_rows
    owns_panel = col_index == row_index // per_column

    def gather(tile):
        return lax.all_gather(tile, "row", axis=0, tiled=True)

    def left_of(full):
        mine = lax.dynamic_slice_in_dim(full, offset, tile_rows, 1)
        return jnp.where(owns_panel, mine, partner(mine, "col", 0))

    def cross(left, full):
        return lax.dot_general(
            left, full, (((0,), (0,)), ((), ())), preferred_element_type=jnp.float32
        )

    current = sigma_end.astype(jnp.bfloat16)
    factor = gather(factors[0])
    state = gather(current)
    inverse = gather(inverses[0])
    factor_left = left_of(factor)
    diagonal = cross(left_of(inverse), inverse)
    result = None
    for segment in range(sec_size):
        half = cross(factor_left, state).astype(jnp.bfloat16)
        whole = lax.all_gather(half, "col", axis=1, tiled=True)
        block = diagonal + jnp.dot(whole, factor, preferred_element_type=jnp.float32)
        active = sec_index == sec_size - 1 - segment
        result = block if result is None else jnp.where(active, block, result)
        if segment < sec_size - 1:
            state = gather(passed_along(block.astype(jnp.bfloat16), "sec", -1))
    return result[None]


FAC, INV, SIG, STA = range(4)
DOWN, UP = range(2)
MESH = pl.DeviceIdType.MESH
TA = (((0,), (0,)), ((), ()))


def kernel(n, f_ref, g_ref, s_ref, out, fb, gb, sb, xb, fl, gl, g0, db, zb, ssem, rsem, hop_s, hop_x, left_s, left_r, end_s, end_r, z_s, z_r):
    r = lax.axis_index("row")
    c = lax.axis_index("col")
    sec = lax.axis_index("sec")
    t = f_ref.shape[1]
    lower, upper = r > 0, r < n - 1
    below = {INV: r > 1}
    bufs = {FAC: fb, INV: gb, SIG: sb, STA: xb}
    lefts = (fl, gl, g0)
    sources = (fb, gb, gb)
    owners = (c == r // 2, c == r // 2, jnp.logical_and(c == 0, r == 1))
    picks = (r % 2, r % 2, 0)
    spans = ((0, t), (0, t // 2), (t // 2, t // 2))

    barrier = pltpu.get_barrier_semaphore()
    pl.semaphore_signal(barrier, inc=1, device_id={"col": 1 - c}, device_id_type=MESH)
    pl.semaphore_signal(barrier, inc=1, device_id={"sec": 1 - sec}, device_id_type=MESH)

    @pl.when(lower)
    def _():
        pl.semaphore_signal(barrier, inc=1, device_id={"row": r - 1}, device_id_type=MESH)

    @pl.when(upper)
    def _():
        pl.semaphore_signal(barrier, inc=1, device_id={"row": r + 1}, device_id_type=MESH)

    pl.semaphore_wait(barrier, 2 + lower.astype(jnp.int32) + upper.astype(jnp.int32))

    def rows(k):
        return pl.ds(pl.multiple_of(k * t, t), t)

    def cols(h):
        return pl.ds(h * t, t)

    def state_piece(p, k):
        first, width = spans[p]
        return xb.at[min(p, 1), rows(k), pl.ds(first, width)]

    def along(a, k, h, way):
        piece = state_piece(h, k) if a == STA else bufs[a].at[h, rows(k), :]
        to = r - 1 if way == DOWN else r + 1
        return pltpu.make_async_remote_copy(
            src_ref=piece,
            dst_ref=piece,
            send_sem=ssem.at[a, h, k, way],
            recv_sem=rsem.at[a, h, k],
            device_id={"row": to},
            device_id_type=MESH,
        )

    def hop_sigma(k):
        piece = sb.at[0, rows(k), :]
        return pltpu.make_async_remote_copy(
            src_ref=piece, dst_ref=piece, send_sem=hop_s.at[k], recv_sem=rsem.at[SIG, 0, k],
            device_id={"sec": 1}, device_id_type=MESH,
        )

    def hop_state(p, k):
        piece = state_piece(p, k)
        return pltpu.make_async_remote_copy(
            src_ref=piece, dst_ref=piece, send_sem=hop_x.at[p, k], recv_sem=rsem.at[STA, p, k],
            device_id={"sec": 0}, device_id_type=MESH,
        )

    def to_left(a, k):
        return pltpu.make_async_remote_copy(
            src_ref=sources[a].at[picks[a], rows(k), :], dst_ref=lefts[a].at[rows(k), :],
            send_sem=left_s.at[a, k], recv_sem=left_r.at[a, k],
            device_id={"col": 1 - c}, device_id_type=MESH,
        )

    def flows(a, k, h, way):
        if a != INV:
            return True
        return (2 * c + h <= k) if way == DOWN else False

    def when(*terms):
        total = True
        for term in terms:
            if term is False or (isinstance(term, bool) and not term):
                return lambda f: None
            if term is not True:
                total = term if total is True else jnp.logical_and(total, term)
        return pl.when(total)

    def start_own(a, h):
        @when(below.get(a, lower), flows(a, r, h, DOWN))
        def _():
            along(a, r, h, DOWN).start()

        @when(upper, flows(a, r, h, UP))
        def _():
            along(a, r, h, UP).start()

    def receive(a, h, d, then=None):
        for way, k, edge in ((DOWN, r + d, below.get(a, lower)), (UP, r - d, upper)):
            @when(k < n if way == DOWN else k >= 0, a != INV or lower, flows(a, k, h, way))
            def _():
                along(a, k, h, way).wait_recv()

                @pl.when(edge)
                def _():
                    along(a, k, h, way).start()

                if then is not None:
                    then(k)

    def finish(a, h, ways=(DOWN, UP)):
        for k in range(n):
            for way in ways:
                side = jnp.logical_and(below.get(a, lower), r <= k) if way == DOWN else jnp.logical_and(upper, r >= k)

                @when(side, flows(a, k, h, way))
                def _():
                    along(a, k, h, way).wait_send()

    def share_left(a, k):
        @pl.when(owners[a])
        def _():
            to_left(a, k).start()
            lefts[a][rows(k), :] = sources[a][picks[a], rows(k), :]

    for h in range(2):
        gb[h, rows(r), :] = g_ref[0, :, cols(h)]
        start_own(INV, h)
    for h in range(2):
        sb[h, rows(r), :] = s_ref[:, cols(h)].astype(jnp.bfloat16)
    start_own(SIG, sec)
    for h in range(2):
        fb[h, rows(r), :] = f_ref[0, :, cols(h)]
        start_own(FAC, h)
    for a in range(3):
        share_left(a, r)

    for k in range(1, n):
        for h in range(2):
            @pl.when(jnp.logical_and(k > r, k < 2 * c + h))
            def _():
                gb[h, rows(k), :] = jnp.zeros((t, t), jnp.bfloat16)

    def pass_sigma(k):
        @pl.when(sec == 0)
        def _():
            hop_sigma(k).start()

    def cross(left, right):
        return lax.dot_general(left, right, TA, preferred_element_type=jnp.float32)

    def end_copy(h):
        return pltpu.make_async_remote_copy(
            src_ref=db.at[0, h], dst_ref=db.at[1, h], send_sem=end_s.at[h], recv_sem=end_r.at[h],
            device_id={"row": 0}, device_id_type=MESH,
        )

    def diagonals():
        for a, least in ((2, 1), (1, None)):
            for k in range(1, n):
                here = r == 1 if a == 2 else jnp.logical_and(lower, r <= k)

                @when(jnp.logical_and(here, c != (0 if a == 2 else r // 2)))
                def _():
                    to_left(a, k).wait_recv()

        @pl.when(r == 1)
        def _():
            for h in range(2):
                db[0, h] = cross(g0[t:, :], gb[h, t:, :]).astype(jnp.bfloat16)
                end_copy(h).start()

        for first in range(1, n):
            @pl.when(r == first)
            def _():
                for h in range(2):
                    out[0, :, cols(h)] = cross(gl[first * t:, :], gb[h, first * t:, :])

    for d in range(1, n):
        for h in range(2):
            receive(INV, h, d)

        @when(lower, r + d < n)
        def _():
            share_left(1, r + d)
            share_left(2, r + d)

        if d == n - 2:
            diagonals()
        receive(SIG, sec, d, pass_sigma)
        for h in range(2):
            receive(FAC, h, d)
        for k, inside in ((r + d, r + d < n), (r - d, r - d >= 0)):
            @pl.when(inside)
            def _():
                share_left(FAC, k)

    @pl.when(jnp.logical_not(owners[0]))
    def _():
        for k in range(n):
            to_left(0, k).wait_recv()

    @pl.when(r == 0)
    def _():
        @pl.when(c == 1)
        def _():
            to_left(1, 0).wait_recv()

        for h in range(2):
            end_copy(h).wait_recv()
            out[0, :, cols(h)] = cross(gl[:t, :], gb[h, :t, :]) + db[1, h].astype(jnp.float32)

    def send_z():
        piece = zb.at[c]
        return pltpu.make_async_remote_copy(
            src_ref=piece, dst_ref=piece, send_sem=z_s, recv_sem=z_r,
            device_id={"col": 1 - c}, device_id_type=MESH,
        )

    def products(buf, then):
        for h in range(2):
            zb[c, :, cols(h)] = cross(fl[...], buf[h]).astype(jnp.bfloat16)
        send_z().start()
        send_z().wait_recv()
        for h in (1, 0):
            total = out[0, :, cols(h)]
            for j in range(2):
                total += jnp.dot(zb[j], fb[h, j * 2 * t:(j + 1) * 2 * t, :], preferred_element_type=jnp.float32)
            out[0, :, cols(h)] = total
            then(h, total)

    @pl.when(sec == 1)
    def _():
        for k in range(n):
            @pl.when(k != r)
            def _():
                hop_sigma(k).wait_recv()

        def onward(h, total):
            xb[h, rows(r), :] = total.astype(jnp.bfloat16)
            if h == 1:
                hop_state(1, r).start()
                start_own(STA, 2)
                hop_state(2, r).start()
            else:
                hop_state(0, r).start()

        products(sb, onward)
        for d in range(1, n):
            receive(STA, 2, d, lambda k: hop_state(2, k).start())
        finish(STA, 2)
        hop_state(0, r).wait_send()
        hop_state(1, r).wait_send()
        for k in range(n):
            hop_state(2, k).wait_send()

    @pl.when(sec == 0)
    def _():
        for p in (1, 0):
            hop_state(p, r).wait_recv()
            start_own(STA, p)
        for d in range(1, n):
            for p in (1, 0):
                receive(STA, p, d)
        for k in range(n):
            hop_state(2, k).wait_recv()
        products(xb, lambda h, total: None)
        for p in range(2):
            finish(STA, p)
        for k in range(n):
            @pl.when(k != r)
            def _():
                hop_sigma(k).wait_send()

    send_z().wait_send()
    finish(SIG, sec)
    for h in range(2):
        finish(FAC, h)
        finish(INV, h, (DOWN,))

    @pl.when(r == 1)
    def _():
        for h in range(2):
            end_copy(h).wait_send()

    for k in range(n):
        @pl.when(owners[0])
        def _():
            to_left(0, k).wait_send()

        @when(jnp.logical_and(owners[1], jnp.logical_and(r <= k, jnp.logical_or(lower, k == 0))))
        def _():
            to_left(1, k).wait_send()

        @when(owners[2], k >= 1)
        def _():
            to_left(2, k).wait_send()


def fused(factors, inverses, sigma_end):
    n = lax.axis_size("row")
    _, t, width = factors.shape
    low = jnp.bfloat16
    dma = pltpu.SemaphoreType.DMA
    vmem = pl.BlockSpec(memory_space=pltpu.VMEM)
    wide = pltpu.VMEM((2, n * t, t), low)
    return pl.pallas_call(
        lambda *refs: kernel(n, *refs),
        out_shape=jax.ShapeDtypeStruct((1, t, width), jnp.float32),
        in_specs=[vmem] * 3,
        out_specs=vmem,
        scratch_shapes=[
            wide, wide, wide, wide,
            pltpu.VMEM((n * t, t), low),
            pltpu.VMEM((n * t, t), low),
            pltpu.VMEM((n * t, t), low),
            pltpu.VMEM((2, 2, t, t), low),
            pltpu.VMEM((2, t, 2 * t), low),
            dma((4, 3, n, 2)), dma((4, 3, n)), dma((n,)), dma((3, n)),
            dma((3, n)), dma((3, n)), dma((2,)), dma((2,)), dma(()), dma(()),
        ],
        compiler_params=pltpu.CompilerParams(
            collective_id=0, has_side_effects=True, vmem_limit_bytes=56 * 2**20
        ),
    )(factors, inverses, sigma_end)


def solution(mesh):
    in_specs = (
        P(("groups", "sec"), "row", "col"),
        P(("groups", "sec"), "row", "col"),
        P(("groups", "row"), "col"),
    )
    fits = mesh.shape["sec"] == 2 and mesh.shape["row"] == 2 * mesh.shape["col"] == 4
    body = fused if fits else local
    out_specs = P(("groups", "sec"), "row", "col")
    return jax.shard_map(body, mesh=mesh, in_specs=in_specs, out_specs=out_specs, check_vma=False)
```

```python
import jax
import jax.numpy as jnp
from jax import lax
from jax.experimental import pallas as pl
from jax.experimental.pallas import tpu as pltpu
from jax.sharding import PartitionSpec as P


def partner(shard, axis, stride):
    return lax.ppermute(shard, axis, [(i, i ^ 1 << stride) for i in range(lax.axis_size(axis))])


def passed_along(value, axis, steps):
    count = lax.axis_size(axis)
    first, last = (max(0, -steps), min(count, count - steps))
    return lax.ppermute(value, axis, [(source, source + steps) for source in range(first, last)])


def local(factors, inverses, sigma_end):
    row_size = lax.axis_size("row")
    col_size = lax.axis_size("col")
    sec_size = lax.axis_size("sec")
    row_index = lax.axis_index("row")
    col_index = lax.axis_index("col")
    sec_index = lax.axis_index("sec")
    _, tile_rows, _ = factors.shape
    per_column = row_size // col_size
    offset = row_index % per_column * tile_rows
    owns_panel = col_index == row_index // per_column

    def gather(tile):
        return lax.all_gather(tile, "row", axis=0, tiled=True)

    def left_of(full):
        mine = lax.dynamic_slice_in_dim(full, offset, tile_rows, 1)
        return jnp.where(owns_panel, mine, partner(mine, "col", 0))

    def cross(left, full):
        return lax.dot_general(
            left, full, (((0,), (0,)), ((), ())), preferred_element_type=jnp.float32
        )

    current = sigma_end.astype(jnp.bfloat16)
    factor = gather(factors[0])
    state = gather(current)
    inverse = gather(inverses[0])
    factor_left = left_of(factor)
    diagonal = cross(left_of(inverse), inverse)
    result = None
    for segment in range(sec_size):
        half = cross(factor_left, state).astype(jnp.bfloat16)
        whole = lax.all_gather(half, "col", axis=1, tiled=True)
        block = diagonal + jnp.dot(whole, factor, preferred_element_type=jnp.float32)
        active = sec_index == sec_size - 1 - segment
        result = block if result is None else jnp.where(active, block, result)
        if segment < sec_size - 1:
            state = gather(passed_along(block.astype(jnp.bfloat16), "sec", -1))
    return result[None]


FAC, INV, SIG, STA = range(4)
DOWN, UP = range(2)
MESH = pl.DeviceIdType.MESH
TA = (((0,), (0,)), ((), ()))


def kernel(n, f_ref, g_ref, s_ref, out, fb, gb, sb, xb, fl, gl, g0, db, zb, zacc, ssem, rsem, hop_s, hop_x, left_s, left_r, end_s, end_r, z_s, z_r):
    r = lax.axis_index("row")
    c = lax.axis_index("col")
    sec = lax.axis_index("sec")
    t = f_ref.shape[1]
    lower, upper = r > 0, r < n - 1
    below = {INV: r > 1}
    bufs = {FAC: fb, INV: gb, SIG: sb, STA: xb}
    lefts = (fl, gl, g0)
    sources = (fb, gb, gb)
    owners = (c == r // 2, c == r // 2, jnp.logical_and(c == 0, r == 1))
    picks = (r % 2, r % 2, 0)
    spans = {
        SIG: ((0, t), (0, t // 2), (t // 2, t // 2)),
        STA: ((0, t), (0, t // 4), (t // 4, t - t // 4)),
    }

    barrier = pltpu.get_barrier_semaphore()
    pl.semaphore_signal(barrier, inc=1, device_id={"col": 1 - c}, device_id_type=MESH)
    pl.semaphore_signal(barrier, inc=1, device_id={"sec": 1 - sec}, device_id_type=MESH)

    @pl.when(lower)
    def _():
        pl.semaphore_signal(barrier, inc=1, device_id={"row": r - 1}, device_id_type=MESH)

    @pl.when(upper)
    def _():
        pl.semaphore_signal(barrier, inc=1, device_id={"row": r + 1}, device_id_type=MESH)

    pl.semaphore_wait(barrier, 2 + lower.astype(jnp.int32) + upper.astype(jnp.int32))

    def rows(k):
        return pl.ds(pl.multiple_of(k * t, t), t)

    def cols(h):
        return pl.ds(h * t, t)

    def piece_of(a, p, k):
        if a not in spans:
            return bufs[a].at[p, rows(k), :]
        first, width = spans[a][p]
        return bufs[a].at[min(p, 1), rows(k), pl.ds(first, width)]

    def along(a, k, h, way):
        piece = piece_of(a, h, k)
        to = r - 1 if way == DOWN else r + 1
        return pltpu.make_async_remote_copy(
            src_ref=piece,
            dst_ref=piece,
            send_sem=ssem.at[a, h, k, way],
            recv_sem=rsem.at[a, h, k],
            device_id={"row": to},
            device_id_type=MESH,
        )

    def hop_sigma(p, k):
        piece = piece_of(SIG, p, k)
        return pltpu.make_async_remote_copy(
            src_ref=piece, dst_ref=piece, send_sem=hop_s.at[p, k], recv_sem=rsem.at[SIG, p, k],
            device_id={"sec": 1}, device_id_type=MESH,
        )

    def hop_state(p, k):
        piece = piece_of(STA, p, k)
        return pltpu.make_async_remote_copy(
            src_ref=piece, dst_ref=piece, send_sem=hop_x.at[p, k], recv_sem=rsem.at[STA, p, k],
            device_id={"sec": 0}, device_id_type=MESH,
        )

    def to_left(a, k):
        return pltpu.make_async_remote_copy(
            src_ref=sources[a].at[picks[a], rows(k), :], dst_ref=lefts[a].at[rows(k), :],
            send_sem=left_s.at[a, k], recv_sem=left_r.at[a, k],
            device_id={"col": 1 - c}, device_id_type=MESH,
        )

    def flows(a, k, h, way):
        if a != INV:
            return True
        return (2 * c + h <= k) if way == DOWN else False

    def when(*terms):
        total = True
        for term in terms:
            if term is False or (isinstance(term, bool) and not term):
                return lambda f: None
            if term is not True:
                total = term if total is True else jnp.logical_and(total, term)
        return pl.when(total)

    def start_own(a, h):
        @when(below.get(a, lower), flows(a, r, h, DOWN))
        def _():
            along(a, r, h, DOWN).start()

        @when(upper, flows(a, r, h, UP))
        def _():
            along(a, r, h, UP).start()

    def receive(a, h, d, then=None):
        for way, k, edge in ((DOWN, r + d, below.get(a, lower)), (UP, r - d, upper)):
            @when(k < n if way == DOWN else k >= 0, a != INV or lower, flows(a, k, h, way))
            def _():
                along(a, k, h, way).wait_recv()

                @pl.when(edge)
                def _():
                    along(a, k, h, way).start()

                if then is not None:
                    then(k)

    def finish(a, h, ways=(DOWN, UP)):
        for k in range(n):
            for way in ways:
                side = jnp.logical_and(below.get(a, lower), r <= k) if way == DOWN else jnp.logical_and(upper, r >= k)

                @when(side, flows(a, k, h, way))
                def _():
                    along(a, k, h, way).wait_send()

    def share_left(a, k):
        @pl.when(owners[a])
        def _():
            to_left(a, k).start()
            lefts[a][rows(k), :] = sources[a][picks[a], rows(k), :]

    for h in range(2):
        sb[h, rows(r), :] = s_ref[:, cols(h)].astype(jnp.bfloat16)

    @pl.when(sec == 0)
    def _():
        start_own(SIG, 0)
        start_own(SIG, 1)

    @pl.when(sec == 1)
    def _():
        start_own(SIG, 2)

    for h in range(2):
        gb[h, rows(r), :] = g_ref[0, :, cols(h)]
        start_own(INV, h)
    for h in range(2):
        fb[h, rows(r), :] = f_ref[0, :, cols(h)]
        start_own(FAC, h)
    for a in range(3):
        share_left(a, r)

    for k in range(1, n):
        for h in range(2):
            @pl.when(jnp.logical_and(k > r, k < 2 * c + h))
            def _():
                gb[h, rows(k), :] = jnp.zeros((t, t), jnp.bfloat16)

    def gather_sigma(d):
        @pl.when(sec == 0)
        def _():
            for p in range(2):
                receive(SIG, p, d, lambda k: hop_sigma(p, k).start())

        @pl.when(sec == 1)
        def _():
            receive(SIG, 2, d)

    def add_rows(buf, k, first=False):
        for h in range(2):
            part = cross(fl[rows(k), :], buf[h, rows(k), :])
            zacc[h] = part if first else zacc[h] + part

    def await_left(k):
        @pl.when(jnp.logical_not(owners[0]))
        def _():
            to_left(0, k).wait_recv()

    def ranked(d, then):
        for k, inside in ((r + d, r + d < n), (r - d, r - d >= 0)):
            @pl.when(inside)
            def _():
                then(k)

    def add_sigma(k, first=False):
        await_left(k)
        if not first:
            for p in range(2):
                hop_sigma(p, k).wait_recv()
        add_rows(sb, k, first)

    def cross(left, right):
        return lax.dot_general(left, right, TA, preferred_element_type=jnp.float32)

    def end_copy(h):
        return pltpu.make_async_remote_copy(
            src_ref=db.at[0, h], dst_ref=db.at[1, h], send_sem=end_s.at[h], recv_sem=end_r.at[h],
            device_id={"row": 0}, device_id_type=MESH,
        )

    def diagonals():
        for a, least in ((2, 1), (1, None)):
            for k in range(1, n):
                here = r == 1 if a == 2 else jnp.logical_and(lower, r <= k)

                @when(jnp.logical_and(here, c != (0 if a == 2 else r // 2)))
                def _():
                    to_left(a, k).wait_recv()

        @pl.when(r == 1)
        def _():
            for h in range(2):
                db[0, h] = cross(g0[t:, :], gb[h, t:, :]).astype(jnp.bfloat16)
                end_copy(h).start()

        for first in range(1, n):
            @pl.when(r == first)
            def _():
                for h in range(2):
                    out[0, :, cols(h)] = cross(gl[first * t:, :], gb[h, first * t:, :])

    for d in range(1, n):
        for h in range(2):
            receive(INV, h, d)

        @when(lower, r + d < n)
        def _():
            share_left(1, r + d)
            share_left(2, r + d)

        if d == n - 2:
            diagonals()
        gather_sigma(d)
        for h in range(2):
            receive(FAC, h, d)
        ranked(d, lambda k: share_left(FAC, k))

        @pl.when(sec == 1)
        def _():
            if d == n - 2:
                add_sigma(r, True)
                for e in range(1, d + 1):
                    ranked(e, add_sigma)
            elif d > n - 2:
                ranked(d, add_sigma)

    @pl.when(sec == 0)
    def _():
        for k in range(n):
            await_left(k)

    @pl.when(r == 0)
    def _():
        @pl.when(c == 1)
        def _():
            to_left(1, 0).wait_recv()

        for h in range(2):
            end_copy(h).wait_recv()
            out[0, :, cols(h)] = cross(gl[:t, :], gb[h, :t, :]) + db[1, h].astype(jnp.float32)

    def send_z(h):
        piece = zb.at[c, :, cols(h)]
        return pltpu.make_async_remote_copy(
            src_ref=piece, dst_ref=piece, send_sem=z_s.at[h], recv_sem=z_r.at[h],
            device_id={"col": 1 - c}, device_id_type=MESH,
        )

    def products(then):
        for h in range(2):
            zb[c, :, cols(h)] = zacc[h].astype(jnp.bfloat16)
            send_z(h).start()
        for h in range(2):
            send_z(h).wait_recv()
        for h in (1, 0):
            total = out[0, :, cols(h)]
            for j in range(2):
                total += jnp.dot(zb[j], fb[h, j * 2 * t:(j + 1) * 2 * t, :], preferred_element_type=jnp.float32)
            out[0, :, cols(h)] = total
            then(h, total)

    @pl.when(sec == 1)
    def _():
        def onward(h, total):
            xb[h, rows(r), :] = total.astype(jnp.bfloat16)
            if h == 1:
                hop_state(1, r).start()
                start_own(STA, 2)
                hop_state(2, r).start()
            else:
                hop_state(0, r).start()

        products(onward)
        for d in range(1, n):
            receive(STA, 2, d, lambda k: hop_state(2, k).start())
        finish(STA, 2)
        hop_state(0, r).wait_send()
        hop_state(1, r).wait_send()
        for k in range(n):
            hop_state(2, k).wait_send()

    def add_state(k, first=False):
        hop_state(2, k).wait_recv()
        add_rows(xb, k, first)

    @pl.when(sec == 0)
    def _():
        for p in (1, 0):
            hop_state(p, r).wait_recv()
            start_own(STA, p)
        for d in range(1, n):
            for p in (1, 0):
                receive(STA, p, d)
            if d == n - 2:
                add_state(r, True)
                for e in range(1, d + 1):
                    ranked(e, add_state)
            elif d > n - 2:
                ranked(d, add_state)
        products(lambda h, total: None)
        for p in range(2):
            finish(STA, p)
        for k in range(n):
            @pl.when(k != r)
            def _():
                for p in range(2):
                    hop_sigma(p, k).wait_send()
        for p in range(2):
            finish(SIG, p)

    @pl.when(sec == 1)
    def _():
        finish(SIG, 2)

    for h in range(2):
        send_z(h).wait_send()
    for h in range(2):
        finish(FAC, h)
        finish(INV, h, (DOWN,))

    @pl.when(r == 1)
    def _():
        for h in range(2):
            end_copy(h).wait_send()

    for k in range(n):
        @pl.when(owners[0])
        def _():
            to_left(0, k).wait_send()

        @when(jnp.logical_and(owners[1], jnp.logical_and(r <= k, jnp.logical_or(lower, k == 0))))
        def _():
            to_left(1, k).wait_send()

        @when(owners[2], k >= 1)
        def _():
            to_left(2, k).wait_send()


def fused(factors, inverses, sigma_end):
    n = lax.axis_size("row")
    _, t, width = factors.shape
    low = jnp.bfloat16
    dma = pltpu.SemaphoreType.DMA
    vmem = pl.BlockSpec(memory_space=pltpu.VMEM)
    wide = pltpu.VMEM((2, n * t, t), low)
    return pl.pallas_call(
        lambda *refs: kernel(n, *refs),
        out_shape=jax.ShapeDtypeStruct((1, t, width), jnp.float32),
        in_specs=[vmem] * 3,
        out_specs=vmem,
        scratch_shapes=[
            wide, wide, wide, wide,
            pltpu.VMEM((n * t, t), low),
            pltpu.VMEM((n * t, t), low),
            pltpu.VMEM((n * t, t), low),
            pltpu.VMEM((2, 2, t, t), low),
            pltpu.VMEM((2, t, 2 * t), low),
            pltpu.VMEM((2, t, t), jnp.float32),
            dma((4, 3, n, 2)), dma((4, 3, n)), dma((2, n)), dma((3, n)),
            dma((3, n)), dma((3, n)), dma((2,)), dma((2,)), dma((2,)), dma((2,)),
        ],
        compiler_params=pltpu.CompilerParams(
            collective_id=0, has_side_effects=True, vmem_limit_bytes=56 * 2**20
        ),
    )(factors, inverses, sigma_end)


def solution(mesh):
    in_specs = (
        P(("groups", "sec"), "row", "col"),
        P(("groups", "sec"), "row", "col"),
        P(("groups", "row"), "col"),
    )
    fits = mesh.shape["sec"] == 2 and mesh.shape["row"] == 2 * mesh.shape["col"] == 4
    body = fused if fits else local
    out_specs = P(("groups", "sec"), "row", "col")
    return jax.shard_map(body, mesh=mesh, in_specs=in_specs, out_specs=out_specs, check_vma=False)
```

```python
import jax
import jax.numpy as jnp
from jax import lax
from jax.experimental import pallas as pl
from jax.experimental.pallas import tpu as pltpu
from jax.sharding import PartitionSpec as P


def partner(shard, axis, stride):
    return lax.ppermute(shard, axis, [(i, i ^ 1 << stride) for i in range(lax.axis_size(axis))])


def passed_along(value, axis, steps):
    count = lax.axis_size(axis)
    first, last = (max(0, -steps), min(count, count - steps))
    return lax.ppermute(value, axis, [(source, source + steps) for source in range(first, last)])


def local(factors, inverses, sigma_end):
    row_size = lax.axis_size("row")
    col_size = lax.axis_size("col")
    sec_size = lax.axis_size("sec")
    row_index = lax.axis_index("row")
    col_index = lax.axis_index("col")
    sec_index = lax.axis_index("sec")
    _, tile_rows, _ = factors.shape
    per_column = row_size // col_size
    offset = row_index % per_column * tile_rows
    owns_panel = col_index == row_index // per_column

    def gather(tile):
        return lax.all_gather(tile, "row", axis=0, tiled=True)

    def left_of(full):
        mine = lax.dynamic_slice_in_dim(full, offset, tile_rows, 1)
        return jnp.where(owns_panel, mine, partner(mine, "col", 0))

    def cross(left, full):
        return lax.dot_general(
            left, full, (((0,), (0,)), ((), ())), preferred_element_type=jnp.float32
        )

    current = sigma_end.astype(jnp.bfloat16)
    factor = gather(factors[0])
    state = gather(current)
    inverse = gather(inverses[0])
    factor_left = left_of(factor)
    diagonal = cross(left_of(inverse), inverse)
    result = None
    for segment in range(sec_size):
        half = cross(factor_left, state).astype(jnp.bfloat16)
        whole = lax.all_gather(half, "col", axis=1, tiled=True)
        block = diagonal + jnp.dot(whole, factor, preferred_element_type=jnp.float32)
        active = sec_index == sec_size - 1 - segment
        result = block if result is None else jnp.where(active, block, result)
        if segment < sec_size - 1:
            state = gather(passed_along(block.astype(jnp.bfloat16), "sec", -1))
    return result[None]


FAC, INV, SIG, STA = range(4)
DOWN, UP = range(2)
MESH = pl.DeviceIdType.MESH
TA = (((0,), (0,)), ((), ()))


def kernel(n, f_ref, g_ref, s_ref, out, fb, gb, sb, xb, fl, gl, g0, db, zb, zacc, ssem, rsem, hop_s, hop_x, left_s, left_r, end_s, end_r, z_s, z_r):
    r = lax.axis_index("row")
    c = lax.axis_index("col")
    sec = lax.axis_index("sec")
    t = f_ref.shape[1]
    lower, upper = r > 0, r < n - 1
    below = {INV: r > 1}
    bufs = {FAC: fb, INV: gb, SIG: sb, STA: xb}
    lefts = (fl, gl, g0)
    sources = (fb, gb, gb)
    owners = (c == r // 2, c == r // 2, jnp.logical_and(c == 0, r == 1))
    picks = (r % 2, r % 2, 0)
    spans = {
        SIG: ((0, t), (0, t // 4), (t // 4, t - t // 4)),
        STA: ((0, t), (0, t // 4), (t // 4, t - t // 4)),
    }

    barrier = pltpu.get_barrier_semaphore()
    pl.semaphore_signal(barrier, inc=1, device_id={"col": 1 - c}, device_id_type=MESH)
    pl.semaphore_signal(barrier, inc=1, device_id={"sec": 1 - sec}, device_id_type=MESH)

    @pl.when(lower)
    def _():
        pl.semaphore_signal(barrier, inc=1, device_id={"row": r - 1}, device_id_type=MESH)

    @pl.when(upper)
    def _():
        pl.semaphore_signal(barrier, inc=1, device_id={"row": r + 1}, device_id_type=MESH)

    pl.semaphore_wait(barrier, 2 + lower.astype(jnp.int32) + upper.astype(jnp.int32))

    def rows(k):
        return pl.ds(pl.multiple_of(k * t, t), t)

    def cols(h):
        return pl.ds(h * t, t)

    def piece_of(a, p, k):
        if a not in spans:
            return bufs[a].at[p, rows(k), :]
        first, width = spans[a][p]
        return bufs[a].at[min(p, 1), rows(k), pl.ds(first, width)]

    def along(a, k, h, way):
        piece = piece_of(a, h, k)
        to = r - 1 if way == DOWN else r + 1
        return pltpu.make_async_remote_copy(
            src_ref=piece,
            dst_ref=piece,
            send_sem=ssem.at[a, h, k, way],
            recv_sem=rsem.at[a, h, k],
            device_id={"row": to},
            device_id_type=MESH,
        )

    def hop_sigma(p, k):
        piece = piece_of(SIG, p, k)
        return pltpu.make_async_remote_copy(
            src_ref=piece, dst_ref=piece, send_sem=hop_s.at[p, k], recv_sem=rsem.at[SIG, p, k],
            device_id={"sec": 1}, device_id_type=MESH,
        )

    def hop_state(p, k):
        piece = piece_of(STA, p, k)
        return pltpu.make_async_remote_copy(
            src_ref=piece, dst_ref=piece, send_sem=hop_x.at[p, k], recv_sem=rsem.at[STA, p, k],
            device_id={"sec": 0}, device_id_type=MESH,
        )

    def to_left(a, k):
        return pltpu.make_async_remote_copy(
            src_ref=sources[a].at[picks[a], rows(k), :], dst_ref=lefts[a].at[rows(k), :],
            send_sem=left_s.at[a, k], recv_sem=left_r.at[a, k],
            device_id={"col": 1 - c}, device_id_type=MESH,
        )

    def flows(a, k, h, way):
        if a != INV:
            return True
        return (2 * c + h <= k) if way == DOWN else False

    def when(*terms):
        total = True
        for term in terms:
            if term is False or (isinstance(term, bool) and not term):
                return lambda f: None
            if term is not True:
                total = term if total is True else jnp.logical_and(total, term)
        return pl.when(total)

    def start_own(a, h):
        @when(below.get(a, lower), flows(a, r, h, DOWN))
        def _():
            along(a, r, h, DOWN).start()

        @when(upper, flows(a, r, h, UP))
        def _():
            along(a, r, h, UP).start()

    def receive(a, h, d, then=None):
        for way, k, edge in ((DOWN, r + d, below.get(a, lower)), (UP, r - d, upper)):
            @when(k < n if way == DOWN else k >= 0, a != INV or lower, flows(a, k, h, way))
            def _():
                along(a, k, h, way).wait_recv()

                @pl.when(edge)
                def _():
                    along(a, k, h, way).start()

                if then is not None:
                    then(k)

    def finish(a, h, ways=(DOWN, UP)):
        for k in range(n):
            for way in ways:
                side = jnp.logical_and(below.get(a, lower), r <= k) if way == DOWN else jnp.logical_and(upper, r >= k)

                @when(side, flows(a, k, h, way))
                def _():
                    along(a, k, h, way).wait_send()

    def share_left(a, k):
        @pl.when(owners[a])
        def _():
            to_left(a, k).start()
            lefts[a][rows(k), :] = sources[a][picks[a], rows(k), :]

    for h in range(2):
        sb[h, rows(r), :] = s_ref[:, cols(h)].astype(jnp.bfloat16)

    for h in range(2):
        gb[h, rows(r), :] = g_ref[0, :, cols(h)]
        fb[h, rows(r), :] = f_ref[0, :, cols(h)]

    def gather_sigma(d):
        for p in range(2):
            receive(SIG, p, d, lambda k: hop_sigma(p, k).start())

    def start_both(a):
        for h in range(2):
            start_own(a, h)

    @pl.when(sec == 0)
    def _():
        start_own(SIG, 0)
        start_own(SIG, 1)
        gather_sigma(1)
        start_both(INV)
        gather_sigma(2)
        start_both(FAC)
        for d in range(3, n):
            gather_sigma(d)

    @pl.when(sec == 1)
    def _():
        start_own(SIG, 2)
        start_both(INV)
        start_both(FAC)

    for a in range(3):
        share_left(a, r)

    for k in range(1, n):
        for h in range(2):
            @pl.when(jnp.logical_and(k > r, k < 2 * c + h))
            def _():
                gb[h, rows(k), :] = jnp.zeros((t, t), jnp.bfloat16)

    def add_rows(buf, k, first=False):
        for h in range(2):
            part = cross(fl[rows(k), :], buf[h, rows(k), :])
            zacc[h] = part if first else zacc[h] + part

    def await_left(k):
        @pl.when(jnp.logical_not(owners[0]))
        def _():
            to_left(0, k).wait_recv()

    def ranked(d, then):
        for k, inside in ((r + d, r + d < n), (r - d, r - d >= 0)):
            @pl.when(inside)
            def _():
                then(k)

    def add_sigma(k, first=False):
        await_left(k)
        if not first:
            for p in range(2):
                hop_sigma(p, k).wait_recv()
        add_rows(sb, k, first)

    def cross(left, right):
        return lax.dot_general(left, right, TA, preferred_element_type=jnp.float32)

    def end_copy(h):
        return pltpu.make_async_remote_copy(
            src_ref=db.at[0, h], dst_ref=db.at[1, h], send_sem=end_s.at[h], recv_sem=end_r.at[h],
            device_id={"row": 0}, device_id_type=MESH,
        )

    def diagonals():
        for a, least in ((2, 1), (1, None)):
            for k in range(1, n):
                here = r == 1 if a == 2 else jnp.logical_and(lower, r <= k)

                @when(jnp.logical_and(here, c != (0 if a == 2 else r // 2)))
                def _():
                    to_left(a, k).wait_recv()

        @pl.when(r == 1)
        def _():
            for h in range(2):
                db[0, h] = cross(g0[t:, :], gb[h, t:, :]).astype(jnp.bfloat16)
                end_copy(h).start()

        for first in range(1, n):
            @pl.when(r == first)
            def _():
                for h in range(2):
                    out[0, :, cols(h)] = cross(gl[first * t:, :], gb[h, first * t:, :])

    for d in range(1, n):
        for h in range(2):
            receive(INV, h, d)

        @when(lower, r + d < n)
        def _():
            share_left(1, r + d)
            share_left(2, r + d)

        if d == n - 2:
            diagonals()
        @pl.when(sec == 1)
        def _():
            receive(SIG, 2, d)

        for h in range(2):
            receive(FAC, h, d)
        ranked(d, lambda k: share_left(FAC, k))

        @pl.when(sec == 1)
        def _():
            if d == n - 2:
                add_sigma(r, True)
                for e in range(1, d + 1):
                    ranked(e, add_sigma)
            elif d > n - 2:
                ranked(d, add_sigma)

    @pl.when(sec == 0)
    def _():
        for k in range(n):
            await_left(k)

    @pl.when(r == 0)
    def _():
        @pl.when(c == 1)
        def _():
            to_left(1, 0).wait_recv()

        for h in range(2):
            end_copy(h).wait_recv()
            out[0, :, cols(h)] = cross(gl[:t, :], gb[h, :t, :]) + db[1, h].astype(jnp.float32)

    def send_z(h):
        piece = zb.at[c, :, cols(h)]
        return pltpu.make_async_remote_copy(
            src_ref=piece, dst_ref=piece, send_sem=z_s.at[h], recv_sem=z_r.at[h],
            device_id={"col": 1 - c}, device_id_type=MESH,
        )

    def products(then):
        for h in range(2):
            zb[c, :, cols(h)] = zacc[h].astype(jnp.bfloat16)
            send_z(h).start()
        for h in range(2):
            send_z(h).wait_recv()
        for h in (1, 0):
            total = out[0, :, cols(h)]
            for j in range(2):
                total += jnp.dot(zb[j], fb[h, j * 2 * t:(j + 1) * 2 * t, :], preferred_element_type=jnp.float32)
            out[0, :, cols(h)] = total
            then(h, total)

    @pl.when(sec == 1)
    def _():
        def onward(h, total):
            xb[h, rows(r), :] = total.astype(jnp.bfloat16)
            if h == 1:
                hop_state(1, r).start()
                start_own(STA, 2)
                hop_state(2, r).start()
            else:
                hop_state(0, r).start()

        products(onward)
        for d in range(1, n):
            receive(STA, 2, d, lambda k: hop_state(2, k).start())
        finish(STA, 2)
        hop_state(0, r).wait_send()
        hop_state(1, r).wait_send()
        for k in range(n):
            hop_state(2, k).wait_send()

    def add_state(k, first=False):
        hop_state(2, k).wait_recv()
        add_rows(xb, k, first)

    @pl.when(sec == 0)
    def _():
        for p in (1, 0):
            hop_state(p, r).wait_recv()
            start_own(STA, p)
        for d in range(1, n):
            for p in (1, 0):
                receive(STA, p, d)
            if d == n - 2:
                add_state(r, True)
                for e in range(1, d + 1):
                    ranked(e, add_state)
            elif d > n - 2:
                ranked(d, add_state)
        products(lambda h, total: None)
        for p in range(2):
            finish(STA, p)
        for k in range(n):
            @pl.when(k != r)
            def _():
                for p in range(2):
                    hop_sigma(p, k).wait_send()
        for p in range(2):
            finish(SIG, p)

    @pl.when(sec == 1)
    def _():
        finish(SIG, 2)

    for h in range(2):
        send_z(h).wait_send()
    for h in range(2):
        finish(FAC, h)
        finish(INV, h, (DOWN,))

    @pl.when(r == 1)
    def _():
        for h in range(2):
            end_copy(h).wait_send()

    for k in range(n):
        @pl.when(owners[0])
        def _():
            to_left(0, k).wait_send()

        @when(jnp.logical_and(owners[1], jnp.logical_and(r <= k, jnp.logical_or(lower, k == 0))))
        def _():
            to_left(1, k).wait_send()

        @when(owners[2], k >= 1)
        def _():
            to_left(2, k).wait_send()


def fused(factors, inverses, sigma_end):
    n = lax.axis_size("row")
    _, t, width = factors.shape
    low = jnp.bfloat16
    dma = pltpu.SemaphoreType.DMA
    vmem = pl.BlockSpec(memory_space=pltpu.VMEM)
    wide = pltpu.VMEM((2, n * t, t), low)
    return pl.pallas_call(
        lambda *refs: kernel(n, *refs),
        out_shape=jax.ShapeDtypeStruct((1, t, width), jnp.float32),
        in_specs=[vmem] * 3,
        out_specs=vmem,
        scratch_shapes=[
            wide, wide, wide, wide,
            pltpu.VMEM((n * t, t), low),
            pltpu.VMEM((n * t, t), low),
            pltpu.VMEM((n * t, t), low),
            pltpu.VMEM((2, 2, t, t), low),
            pltpu.VMEM((2, t, 2 * t), low),
            pltpu.VMEM((2, t, t), jnp.float32),
            dma((4, 3, n, 2)), dma((4, 3, n)), dma((2, n)), dma((3, n)),
            dma((3, n)), dma((3, n)), dma((2,)), dma((2,)), dma((2,)), dma((2,)),
        ],
        compiler_params=pltpu.CompilerParams(
            collective_id=0, has_side_effects=True, vmem_limit_bytes=56 * 2**20
        ),
    )(factors, inverses, sigma_end)


def solution(mesh):
    in_specs = (
        P(("groups", "sec"), "row", "col"),
        P(("groups", "sec"), "row", "col"),
        P(("groups", "row"), "col"),
    )
    fits = mesh.shape["sec"] == 2 and mesh.shape["row"] == 2 * mesh.shape["col"] == 4
    body = fused if fits else local
    out_specs = P(("groups", "sec"), "row", "col")
    return jax.shard_map(body, mesh=mesh, in_specs=in_specs, out_specs=out_specs, check_vma=False)
```

```python
import jax
import jax.numpy as jnp
from jax import lax
from jax.experimental import pallas as pl
from jax.experimental.pallas import tpu as pltpu
from jax.sharding import PartitionSpec as P


def partner(shard, axis, stride):
    return lax.ppermute(shard, axis, [(i, i ^ 1 << stride) for i in range(lax.axis_size(axis))])


def passed_along(value, axis, steps):
    count = lax.axis_size(axis)
    first, last = (max(0, -steps), min(count, count - steps))
    return lax.ppermute(value, axis, [(source, source + steps) for source in range(first, last)])


def local(factors, inverses, sigma_end):
    row_size = lax.axis_size("row")
    col_size = lax.axis_size("col")
    sec_size = lax.axis_size("sec")
    row_index = lax.axis_index("row")
    col_index = lax.axis_index("col")
    sec_index = lax.axis_index("sec")
    _, tile_rows, _ = factors.shape
    per_column = row_size // col_size
    offset = row_index % per_column * tile_rows
    owns_panel = col_index == row_index // per_column

    def gather(tile):
        return lax.all_gather(tile, "row", axis=0, tiled=True)

    def left_of(full):
        mine = lax.dynamic_slice_in_dim(full, offset, tile_rows, 1)
        return jnp.where(owns_panel, mine, partner(mine, "col", 0))

    def cross(left, full):
        return lax.dot_general(
            left, full, (((0,), (0,)), ((), ())), preferred_element_type=jnp.float32
        )

    current = sigma_end.astype(jnp.bfloat16)
    factor = gather(factors[0])
    state = gather(current)
    inverse = gather(inverses[0])
    factor_left = left_of(factor)
    diagonal = cross(left_of(inverse), inverse)
    result = None
    for segment in range(sec_size):
        half = cross(factor_left, state).astype(jnp.bfloat16)
        whole = lax.all_gather(half, "col", axis=1, tiled=True)
        block = diagonal + jnp.dot(whole, factor, preferred_element_type=jnp.float32)
        active = sec_index == sec_size - 1 - segment
        result = block if result is None else jnp.where(active, block, result)
        if segment < sec_size - 1:
            state = gather(passed_along(block.astype(jnp.bfloat16), "sec", -1))
    return result[None]


FAC, INV, SIG, STA = range(4)
DOWN, UP = range(2)
MESH = pl.DeviceIdType.MESH
TA = (((0,), (0,)), ((), ()))


def kernel(n, f_ref, g_ref, s_ref, out, fb, gb, sb, xb, fl, gl, g0, db, zb, zacc, ssem, rsem, hop_s, hop_x, left_s, left_r, end_s, end_r, z_s, z_r):
    r = lax.axis_index("row")
    c = lax.axis_index("col")
    sec = lax.axis_index("sec")
    t = f_ref.shape[1]
    lower, upper = r > 0, r < n - 1
    below = {INV: r > 1}
    bufs = {FAC: fb, INV: gb, SIG: sb, STA: xb}
    lefts = (fl, gl, g0)
    sources = (fb, gb, gb)
    owners = (c == r // 2, c == r // 2, jnp.logical_and(c == 0, r == 1))
    picks = (r % 2, r % 2, 0)
    spans = {
        SIG: ((0, t), (0, t // 4), (t // 4, t - t // 4)),
        STA: ((0, t), (0, t // 4), (t // 4, t - t // 4)),
    }

    barrier = pltpu.get_barrier_semaphore()
    pl.semaphore_signal(barrier, inc=1, device_id={"col": 1 - c}, device_id_type=MESH)
    pl.semaphore_signal(barrier, inc=1, device_id={"sec": 1 - sec}, device_id_type=MESH)

    @pl.when(lower)
    def _():
        pl.semaphore_signal(barrier, inc=1, device_id={"row": r - 1}, device_id_type=MESH)

    @pl.when(upper)
    def _():
        pl.semaphore_signal(barrier, inc=1, device_id={"row": r + 1}, device_id_type=MESH)

    pl.semaphore_wait(barrier, 2 + lower.astype(jnp.int32) + upper.astype(jnp.int32))

    def rows(k):
        return pl.ds(pl.multiple_of(k * t, t), t)

    def cols(h):
        return pl.ds(h * t, t)

    def piece_of(a, p, k):
        if a not in spans:
            return bufs[a].at[p, rows(k), :]
        first, width = spans[a][p]
        return bufs[a].at[min(p, 1), rows(k), pl.ds(first, width)]

    def along(a, k, h, way):
        piece = piece_of(a, h, k)
        to = r - 1 if way == DOWN else r + 1
        return pltpu.make_async_remote_copy(
            src_ref=piece,
            dst_ref=piece,
            send_sem=ssem.at[a, h, k, way],
            recv_sem=rsem.at[a, h, k],
            device_id={"row": to},
            device_id_type=MESH,
        )

    def hop_sigma(p, k):
        piece = piece_of(SIG, p, k)
        return pltpu.make_async_remote_copy(
            src_ref=piece, dst_ref=piece, send_sem=hop_s.at[p, k], recv_sem=rsem.at[SIG, p, k],
            device_id={"sec": 1}, device_id_type=MESH,
        )

    def hop_state(p, k):
        piece = piece_of(STA, p, k)
        return pltpu.make_async_remote_copy(
            src_ref=piece, dst_ref=piece, send_sem=hop_x.at[p, k], recv_sem=rsem.at[STA, p, k],
            device_id={"sec": 0}, device_id_type=MESH,
        )

    def to_left(a, k):
        return pltpu.make_async_remote_copy(
            src_ref=sources[a].at[picks[a], rows(k), :], dst_ref=lefts[a].at[rows(k), :],
            send_sem=left_s.at[a, k], recv_sem=left_r.at[a, k],
            device_id={"col": 1 - c}, device_id_type=MESH,
        )

    def flows(a, k, h, way):
        if a != INV:
            return True
        return (2 * c + h <= k) if way == DOWN else False

    def when(*terms):
        total = True
        for term in terms:
            if term is False or (isinstance(term, bool) and not term):
                return lambda f: None
            if term is not True:
                total = term if total is True else jnp.logical_and(total, term)
        return pl.when(total)

    def start_own(a, h):
        @when(below.get(a, lower), flows(a, r, h, DOWN))
        def _():
            along(a, r, h, DOWN).start()

        @when(upper, flows(a, r, h, UP))
        def _():
            along(a, r, h, UP).start()

    def receive(a, h, d, then=None):
        for way, k, edge in ((DOWN, r + d, below.get(a, lower)), (UP, r - d, upper)):
            @when(k < n if way == DOWN else k >= 0, a != INV or lower, flows(a, k, h, way))
            def _():
                along(a, k, h, way).wait_recv()

                @pl.when(edge)
                def _():
                    along(a, k, h, way).start()

                if then is not None:
                    then(k)

    def finish(a, h, ways=(DOWN, UP)):
        for k in range(n):
            for way in ways:
                side = jnp.logical_and(below.get(a, lower), r <= k) if way == DOWN else jnp.logical_and(upper, r >= k)

                @when(side, flows(a, k, h, way))
                def _():
                    along(a, k, h, way).wait_send()

    def share_left(a, k):
        @pl.when(owners[a])
        def _():
            to_left(a, k).start()
            lefts[a][rows(k), :] = sources[a][picks[a], rows(k), :]

    for h in range(2):
        sb[h, rows(r), :] = s_ref[:, cols(h)].astype(jnp.bfloat16)

    for h in range(2):
        gb[h, rows(r), :] = g_ref[0, :, cols(h)]
        fb[h, rows(r), :] = f_ref[0, :, cols(h)]

    def gather_sigma(d):
        for p in range(2):
            receive(SIG, p, d, lambda k: hop_sigma(p, k).start())

    def start_both(a):
        for h in range(2):
            start_own(a, h)

    @pl.when(sec == 0)
    def _():
        start_own(SIG, 0)
        start_own(SIG, 1)
        gather_sigma(1)
        start_both(INV)
        gather_sigma(2)
        start_both(FAC)
        for d in range(3, n):
            gather_sigma(d)

    @pl.when(sec == 1)
    def _():
        start_own(SIG, 2)
        start_both(INV)
        start_both(FAC)

    for a in range(3):
        share_left(a, r)

    for k in range(1, n):
        for h in range(2):
            @pl.when(jnp.logical_and(k > r, k < 2 * c + h))
            def _():
                gb[h, rows(k), :] = jnp.zeros((t, t), jnp.bfloat16)

    def add_rows(buf, k, first=False):
        for h in range(2):
            part = cross(fl[rows(k), :], buf[h, rows(k), :])
            zacc[h] = part if first else zacc[h] + part

    def await_left(k):
        @pl.when(jnp.logical_not(owners[0]))
        def _():
            to_left(0, k).wait_recv()

    def ranked(d, then):
        for k, inside in ((r + d, r + d < n), (r - d, r - d >= 0)):
            @pl.when(inside)
            def _():
                then(k)

    def add_sigma(k, first=False):
        await_left(k)
        if not first:
            for p in range(2):
                hop_sigma(p, k).wait_recv()
        add_rows(sb, k, first)

    def cross(left, right):
        return lax.dot_general(left, right, TA, preferred_element_type=jnp.float32)

    def end_copy(h):
        return pltpu.make_async_remote_copy(
            src_ref=db.at[0, h], dst_ref=db.at[1, h], send_sem=end_s.at[h], recv_sem=end_r.at[h],
            device_id={"row": 0}, device_id_type=MESH,
        )

    def diagonals():
        for a, least in ((2, 1), (1, None)):
            for k in range(1, n):
                here = r == 1 if a == 2 else jnp.logical_and(lower, r <= k)

                @when(jnp.logical_and(here, c != (0 if a == 2 else r // 2)))
                def _():
                    to_left(a, k).wait_recv()

        @pl.when(r == 1)
        def _():
            for h in range(2):
                db[0, h] = cross(g0[t:, :], gb[h, t:, :]).astype(jnp.bfloat16)
                end_copy(h).start()

        for first in range(1, n):
            @pl.when(r == first)
            def _():
                for h in range(2):
                    out[0, :, cols(h)] = cross(gl[first * t:, :], gb[h, first * t:, :])

    for d in range(1, n):
        for h in range(2):
            receive(INV, h, d)

        @when(lower, r + d < n)
        def _():
            share_left(1, r + d)
            share_left(2, r + d)

        if d == n - 2:
            diagonals()
        @pl.when(sec == 1)
        def _():
            receive(SIG, 2, d)

        if d == n - 1:
            @pl.when(sec == 0)
            def _():
                for p in (1, 0):
                    hop_state(p, r).wait_recv()
                    start_own(STA, p)

        for h in range(2):
            receive(FAC, h, d)
        ranked(d, lambda k: share_left(FAC, k))

        @pl.when(sec == 1)
        def _():
            if d == n - 2:
                add_sigma(r, True)
                for e in range(1, d + 1):
                    ranked(e, add_sigma)
            elif d > n - 2:
                ranked(d, add_sigma)

    @pl.when(sec == 0)
    def _():
        for k in range(n):
            await_left(k)

    @pl.when(r == 0)
    def _():
        @pl.when(c == 1)
        def _():
            to_left(1, 0).wait_recv()

        for h in range(2):
            end_copy(h).wait_recv()
            out[0, :, cols(h)] = cross(gl[:t, :], gb[h, :t, :]) + db[1, h].astype(jnp.float32)

    def send_z(h):
        piece = zb.at[c, :, cols(h)]
        return pltpu.make_async_remote_copy(
            src_ref=piece, dst_ref=piece, send_sem=z_s.at[h], recv_sem=z_r.at[h],
            device_id={"col": 1 - c}, device_id_type=MESH,
        )

    def products(then):
        for h in range(2):
            zb[c, :, cols(h)] = zacc[h].astype(jnp.bfloat16)
            send_z(h).start()
        for h in range(2):
            send_z(h).wait_recv()
        for h in (1, 0):
            total = out[0, :, cols(h)]
            for j in range(2):
                total += jnp.dot(zb[j], fb[h, j * 2 * t:(j + 1) * 2 * t, :], preferred_element_type=jnp.float32)
            out[0, :, cols(h)] = total
            then(h, total)

    @pl.when(sec == 1)
    def _():
        def onward(h, total):
            xb[h, rows(r), :] = total.astype(jnp.bfloat16)
            if h == 1:
                hop_state(1, r).start()
                start_own(STA, 2)
            else:
                hop_state(0, r).start()
                hop_state(2, r).start()

        products(onward)
        for d in range(1, n):
            receive(STA, 2, d, lambda k: hop_state(2, k).start())
        finish(STA, 2)
        hop_state(0, r).wait_send()
        hop_state(1, r).wait_send()
        for k in range(n):
            hop_state(2, k).wait_send()

    def add_state(k, first=False):
        hop_state(2, k).wait_recv()
        add_rows(xb, k, first)

    @pl.when(sec == 0)
    def _():
        for d in range(1, n):
            for p in (1, 0):
                receive(STA, p, d)
            if d == n - 2:
                add_state(r, True)
                for e in range(1, d + 1):
                    ranked(e, add_state)
            elif d > n - 2:
                ranked(d, add_state)
        products(lambda h, total: None)
        for p in range(2):
            finish(STA, p)
        for k in range(n):
            @pl.when(k != r)
            def _():
                for p in range(2):
                    hop_sigma(p, k).wait_send()
        for p in range(2):
            finish(SIG, p)

    @pl.when(sec == 1)
    def _():
        finish(SIG, 2)

    for h in range(2):
        send_z(h).wait_send()
    for h in range(2):
        finish(FAC, h)
        finish(INV, h, (DOWN,))

    @pl.when(r == 1)
    def _():
        for h in range(2):
            end_copy(h).wait_send()

    for k in range(n):
        @pl.when(owners[0])
        def _():
            to_left(0, k).wait_send()

        @when(jnp.logical_and(owners[1], jnp.logical_and(r <= k, jnp.logical_or(lower, k == 0))))
        def _():
            to_left(1, k).wait_send()

        @when(owners[2], k >= 1)
        def _():
            to_left(2, k).wait_send()


def fused(factors, inverses, sigma_end):
    n = lax.axis_size("row")
    _, t, width = factors.shape
    low = jnp.bfloat16
    dma = pltpu.SemaphoreType.DMA
    vmem = pl.BlockSpec(memory_space=pltpu.VMEM)
    wide = pltpu.VMEM((2, n * t, t), low)
    return pl.pallas_call(
        lambda *refs: kernel(n, *refs),
        out_shape=jax.ShapeDtypeStruct((1, t, width), jnp.float32),
        in_specs=[vmem] * 3,
        out_specs=vmem,
        scratch_shapes=[
            wide, wide, wide, wide,
            pltpu.VMEM((n * t, t), low),
            pltpu.VMEM((n * t, t), low),
            pltpu.VMEM((n * t, t), low),
            pltpu.VMEM((2, 2, t, t), low),
            pltpu.VMEM((2, t, 2 * t), low),
            pltpu.VMEM((2, t, t), jnp.float32),
            dma((4, 3, n, 2)), dma((4, 3, n)), dma((2, n)), dma((3, n)),
            dma((3, n)), dma((3, n)), dma((2,)), dma((2,)), dma((2,)), dma((2,)),
        ],
        compiler_params=pltpu.CompilerParams(
            collective_id=0, has_side_effects=True, vmem_limit_bytes=56 * 2**20
        ),
    )(factors, inverses, sigma_end)


def solution(mesh):
    in_specs = (
        P(("groups", "sec"), "row", "col"),
        P(("groups", "sec"), "row", "col"),
        P(("groups", "row"), "col"),
    )
    fits = mesh.shape["sec"] == 2 and mesh.shape["row"] == 2 * mesh.shape["col"] == 4
    body = fused if fits else local
    out_specs = P(("groups", "sec"), "row", "col")
    return jax.shard_map(body, mesh=mesh, in_specs=in_specs, out_specs=out_specs, check_vma=False)
```
